32 devices in a mesh: dp: 4 (over y, x), seq: 4 (over z), tensor: 2 (over core).
Axes of the slice: x: 2, y: 2, z: 4, core: 2. Of those that a mesh axis runs over, the one named last changes fastest.
Arguments:
- block_input: bfloat16 [4096, 2560], P(('dp', 'seq')), may hold values from -6 to 6
- seq_ids: int32 [4, 1024], P('dp'), may hold values from 0 to 2, never falling along the last dimension, each value on 1 to 512 neighbouring positions
- out_cotangent: float32 [4096, 2560], P(('dp', 'seq')), may hold values from -6 to 6
- rec_norm_gain: bfloat16 [2560], P('dp'), may hold values from 0.5 to 1.5
- lru_in_weight: bfloat16 [2560, 1536], P('dp', 'tensor'), may hold values from -0.125 to 0.125
- gelu_in_weight: bfloat16 [2560, 1536], P('dp', 'tensor'), may hold values from -0.125 to 0.125
- conv_weight: bfloat16 [4, 6, 256], P(None, 'tensor', 'dp'), may hold values from -3 to 3
- gate_a_weight: bfloat16 [6, 256, 256], P('tensor', 'dp'), may hold values from -0.375 to 0.375
- gate_x_weight: bfloat16 [6, 256, 256], P('tensor', 'dp'), may hold values from -0.375 to 0.375
- decay_param: bfloat16 [6, 256], P('tensor', 'dp'), may hold values from -7 to -1
- lru_out_weight: bfloat16 [1536, 2560], P('tensor', 'dp'), may hold values from -0.3125 to 0.3125
- rec_mlp_gain: bfloat16 [2560], P('dp'), may hold values from 0.5 to 1.5
- rec_mlp_gate: bfloat16 [2560, 3840], P('dp', 'tensor'), may hold values from -0.125 to 0.125
- rec_mlp_up: bfloat16 [2560, 3840], P('dp', 'tensor'), may hold values from -0.125 to 0.125
- rec_mlp_down: bfloat16 [3840, 2560], P('tensor', 'dp'), may hold values from -0.125 to 0.125
- att_norm_gain: bfloat16 [2560], P('dp'), may hold values from 0.5 to 1.5
- query_weight: bfloat16 [2560, 1536], P('dp', 'tensor'), may hold values from -0.125 to 0.125
- key_weight: bfloat16 [2560, 256], P('dp'), may hold values from -0.125 to 0.125
- value_weight: bfloat16 [2560, 256], P('dp'), may hold values from -0.125 to 0.125
- att_out_weight: bfloat16 [1536, 2560], P('tensor', 'dp'), may hold values from -0.625 to 0.625
- att_mlp_gain: bfloat16 [2560], P('dp'), may hold values from 0.5 to 1.5
- att_mlp_gate: bfloat16 [2560, 3840], P('dp', 'tensor'), may hold values from -0.125 to 0.125
- att_mlp_up: bfloat16 [2560, 3840], P('dp', 'tensor'), may hold values from -0.125 to 0.125
- att_mlp_down: bfloat16 [3840, 2560], P('tensor', 'dp'), may hold values from -0.125 to 0.125
Outputs:
- block_output: bfloat16 [4096, 2560], P(('dp', 'seq'))
- input_grad: float32 [4096, 2560], P(('dp', 'seq'))
- grad_rec_norm_gain: float32 [2560], P('dp')
- grad_lru_in_weight: float32 [2560, 1536], P('dp', 'tensor')
- grad_gelu_in_weight: float32 [2560, 1536], P('dp', 'tensor')
- grad_conv_weight: float32 [4, 6, 256], P(None, 'tensor', 'dp')
- grad_gate_a_weight: float32 [6, 256, 256], P('tensor', 'dp')
- grad_gate_x_weight: float32 [6, 256, 256], P('tensor', 'dp')
- grad_decay_param: float32 [6, 256], P('tensor', 'dp')
- grad_lru_out_weight: float32 [1536, 2560], P('tensor', 'dp')
- grad_rec_mlp_gain: float32 [2560], P('dp')
- grad_rec_mlp_gate: float32 [2560, 3840], P('dp', 'tensor')
- grad_rec_mlp_up: float32 [2560, 3840], P('dp', 'tensor')
- grad_rec_mlp_down: float32 [3840, 2560], P('tensor', 'dp')
- grad_att_norm_gain: float32 [2560], P('dp')
- grad_query_weight: float32 [2560, 1536], P('dp', 'tensor')
- grad_key_weight: float32 [2560, 256], P('dp')
- grad_value_weight: float32 [2560, 256], P('dp')
- grad_att_out_weight: float32 [1536, 2560], P('tensor', 'dp')
- grad_att_mlp_gain: float32 [2560], P('dp')
- grad_att_mlp_gate: float32 [2560, 3840], P('dp', 'tensor')
- grad_att_mlp_up: float32 [2560, 3840], P('dp', 'tensor')
- grad_att_mlp_down: float32 [3840, 2560], P('tensor', 'dp')
The draws below stay inside these ranges and needn't reach their ends.
Inputs may be any that keep to these rules, and one draw needn't show every extreme that they name: `seq_ids`: each row is one data group's stream of 1024 tokens in 3 sequences: sequence numbers start at 0 and never fall, every sequence has 1 to 512 tokens and one has exactly 512.
All inputs are finite; a program needn't handle non-finite values.
Results may differ from the reference program's by a relative error of at most 0.04.
Values may be sent and summed in bfloat16 or wider, within the bound.
No kernel may reach another device: no remote copies, remote signals or barrier semaphores. Data moves between devices by JAX's collectives and lax.ppermute only.
A program may use at most 448 MiB of HBM per device.

```python
import math
import jax
import jax.numpy as jnp
import numpy as np
from jax import lax

D = 2560
BLOCKS = 6
BW = 256
R = 1536
HS = 256
QW = 1536
FF = 3840
TAPS = 4
SEGS = 3
S = 1024
MOST = 512
TOKENS = 4096
N_DP = 4


def block_scale(own_key, extent, split, smallest, high):
    factor_of, own = 1.0, jax.random.fold_in(own_key, 6)
    for axis_at, parts in split:
        draws = jnp.exp(jax.random.uniform(jax.random.fold_in(own, axis_at), (parts,), jnp.float32, smallest / len(split), high / len(split)))
        factor_of = factor_of * jnp.repeat(draws, extent[axis_at] // parts).reshape([-1 if axis == axis_at else 1 for axis in range(len(extent))])
    return factor_of


def split_up(amount, total, reach, lean):
    portions = [(1 << 20) // math.isqrt(rank ** lean) + 1 for rank in range(2, amount + 1)]
    spare, given = total - reach - (amount - 1), [1] * (amount - 1)
    while spare > 0:
        free = [i for i in range(amount - 1) if given[i] < reach]
        pool, left = sum([portions[i] for i in free]), spare
        for i in free:
            addition = min(reach - given[i], max(1, left * portions[i] // pool), spare)
            given[i] = given[i] + addition
            spare = spare - addition
    return np.array([reach] + given)


def ragged(stream_key, amount, total, limit, slope):
    if amount == 2:
        one = jax.random.randint(stream_key, (), max(1, total - limit), min(limit, total - 1) + 1)
        return jnp.stack([one, total - one])
    lengths = jnp.asarray(split_up(amount, total, limit, slope), jnp.int32)
    pairs = (amount - 1) // 2
    source_of, taker = lengths[1:1 + 2 * pairs:2], lengths[2:2 + 2 * pairs:2]
    slack = jnp.minimum(source_of - 1, limit - taker)
    passed = jax.random.randint(jax.random.fold_in(stream_key, 1), (pairs,), 0, 1 << 20) % (slack + 1)
    lengths = lengths.at[1:1 + 2 * pairs:2].set(source_of - passed).at[2:2 + 2 * pairs:2].set(taker + passed)
    return lengths[jax.random.permutation(jax.random.fold_in(stream_key, 2), amount)]


def normal_values(own_key, extent, deviation, limit, pieces=(), held_as=jnp.bfloat16):
    array = jax.random.normal(own_key, extent, jnp.float32) * deviation
    if len(pieces) > 0:
        array = block_scale(own_key, extent, pieces, -0.22, 0.18) * array
    return jnp.clip(array, min=-limit, max=limit).astype(held_as)


def setup_inputs(seed: int = 0) -> dict:
    streams_of = jax.random.split(jax.random.key(seed), 25)
    return {
        "block_input": normal_values(streams_of[0], (TOKENS, D), 1.0, 6.0, ((0, 16),)),
        "seq_ids": jax.vmap(lambda own: jnp.searchsorted(jnp.cumsum(ragged(own, SEGS, S, MOST, 2)), jnp.arange(S), side="right"))(jax.random.split(streams_of[1], N_DP)).reshape((N_DP, S)).astype(jnp.int32),
        "out_cotangent": normal_values(streams_of[2], (TOKENS, D), 1.0, 6.0, ((0, 16),), jnp.float32),
        "rec_norm_gain": jnp.clip(1.0 + 0.1 * jax.random.normal(streams_of[3], (D,), jnp.float32), 0.5, 1.5).astype(jnp.bfloat16),
        "lru_in_weight": normal_values(streams_of[4], (D, R), D ** -0.5, 0.125, ((0, 4), (1, 2))),
        "gelu_in_weight": normal_values(streams_of[5], (D, R), D ** -0.5, 0.125, ((0, 4), (1, 2))),
        "conv_weight": normal_values(streams_of[6], (TAPS, BLOCKS, BW), TAPS ** -0.5, 3.0, ((1, 2), (2, 4))),
        "gate_a_weight": normal_values(streams_of[7], (BLOCKS, BW, BW), BW ** -0.5, 0.375, ((0, 2), (1, 4))),
        "gate_x_weight": normal_values(streams_of[8], (BLOCKS, BW, BW), BW ** -0.5, 0.375, ((0, 2), (1, 4))),
        "decay_param": jnp.clip(-7.0 + 6.0 * jax.random.uniform(streams_of[9], (BLOCKS, BW), jnp.float32) ** block_scale(streams_of[9], (BLOCKS, BW), ((0, 2), (1, 4)), -0.2, 0.2), -7.0, -1.0).astype(jnp.bfloat16),
        "lru_out_weight": normal_values(streams_of[10], (R, D), (R // 4) ** -0.5, 0.3125, ((0, 2), (1, 4))),
        "rec_mlp_gain": jnp.clip(1.0 + 0.1 * jax.random.normal(streams_of[11], (D,), jnp.float32), 0.5, 1.5).astype(jnp.bfloat16),
        "rec_mlp_gate": normal_values(streams_of[12], (D, FF), D ** -0.5, 0.125, ((0, 4), (1, 2))),
        "rec_mlp_up": normal_values(streams_of[13], (D, FF), D ** -0.5, 0.125, ((0, 4), (1, 2))),
        "rec_mlp_down": normal_values(streams_of[14], (FF, D), (FF // 2) ** -0.5, 0.125, ((0, 2), (1, 4))),
        "att_norm_gain": jnp.clip(1.0 + 0.1 * jax.random.normal(streams_of[15], (D,), jnp.float32), 0.5, 1.5).astype(jnp.bfloat16),
        "query_weight": normal_values(streams_of[16], (D, QW), D ** -0.5, 0.125, ((0, 4), (1, 2))),
        "key_weight": normal_values(streams_of[17], (D, HS), D ** -0.5, 0.125, ((0, 4),)),
        "value_weight": normal_values(streams_of[18], (D, HS), D ** -0.5, 0.125, ((0, 4),)),
        "att_out_weight": normal_values(streams_of[19], (QW, D), (QW // 16) ** -0.5, 0.625, ((0, 2), (1, 4))),
        "att_mlp_gain": jnp.clip(1.0 + 0.1 * jax.random.normal(streams_of[20], (D,), jnp.float32), 0.5, 1.5).astype(jnp.bfloat16),
        "att_mlp_gate": normal_values(streams_of[21], (D, FF), D ** -0.5, 0.125, ((0, 4), (1, 2))),
        "att_mlp_up": normal_values(streams_of[22], (D, FF), D ** -0.5, 0.125, ((0, 4), (1, 2))),
        "att_mlp_down": normal_values(streams_of[23], (FF, D), (FF // 2) ** -0.5, 0.125, ((0, 2), (1, 4))),
    }


norm_epsilon = 1e-06

def matmul(left, right):
    return jnp.dot(left, right, preferred_element_type=jnp.float32)

def gelu_fn(values):
    return jax.nn.gelu(values, approximate=True)

def gelu_slope(values):
    return jax.vjp(gelu_fn, values)[1](jnp.ones_like(values))[0]

def norm_forward(stream, norm_gain):
    inv_rms = lax.rsqrt(lax.optimization_barrier(jnp.mean(stream * stream, axis=-1, keepdims=True)) + norm_epsilon)
    return ((stream * inv_rms * norm_gain.astype(jnp.float32)).astype(jnp.bfloat16), inv_rms)

def norm_backward(stream, inv_rms, norm_gain, grad_normed):
    weighted = grad_normed * norm_gain.astype(jnp.float32)
    grad_gain = lax.optimization_barrier(jnp.sum(grad_normed * stream * inv_rms, axis=0))
    cubed = inv_rms * inv_rms * inv_rms
    grad_stream = inv_rms * weighted - stream * cubed * lax.optimization_barrier(jnp.mean(weighted * stream, axis=-1, keepdims=True))
    return (grad_stream, grad_gain)

def positions(seq_row):
    token_index = jnp.arange(seq_row.shape[0], dtype=jnp.int32)
    earlier = jnp.concatenate([(seq_row[:1] - 1).astype(jnp.int32), seq_row[:-1].astype(jnp.int32)])
    seg_first = jnp.where(seq_row != earlier, token_index, jnp.zeros_like(token_index))
    return token_index - lax.cummax(seg_first, axis=0)

def rope_tables(pos_row, head_size):
    half_size = head_size // 2
    freqs = jnp.exp(-jnp.log(10000.0) * (2.0 * jnp.arange(half_size).astype(jnp.float32) / head_size))
    angles = pos_row.astype(jnp.float32)[:, None] * freqs[None, :]
    return (jnp.cos(angles), jnp.sin(angles))

def rotate(vectors, cosine, sine_part):
    half_size = vectors.shape[-1] // 2
    first_half = vectors[..., :half_size]
    second_half = vectors[..., half_size:]
    cos_b = cosine[:, None, :]
    sin_b = sine_part[:, None, :]
    return jnp.concatenate([first_half * cos_b - second_half * sin_b, second_half * cos_b + first_half * sin_b], axis=-1)

def chain(first_pair, second_pair):
    return (first_pair[0] * second_pair[0], second_pair[0] * first_pair[1] + second_pair[1])

def linear_scan(decays, values):
    return lax.associative_scan(chain, (decays, values), axis=0)

def mlp_forward(stream, norm_gain, gate_w, up_w, down_w):
    normed, inv_rms = norm_forward(stream, norm_gain)
    gate_pre = matmul(normed, gate_w)
    up_pre = matmul(normed, up_w)
    hidden = (gelu_fn(gate_pre) * up_pre).astype(jnp.bfloat16)
    return (stream + matmul(hidden, down_w), (normed, inv_rms, gate_pre, up_pre, hidden))

def mlp_backward(grad_stream, stream, saved, norm_gain, gate_w, up_w, down_w):
    normed, inv_rms, gate_pre, up_pre, hidden = saved
    grad_low = grad_stream.astype(jnp.bfloat16)
    grad_down = matmul(hidden.T, grad_low)
    grad_hidden = matmul(grad_low, down_w.T)
    grad_gate = (grad_hidden * up_pre * gelu_slope(gate_pre)).astype(jnp.bfloat16)
    grad_up = (grad_hidden * gelu_fn(gate_pre)).astype(jnp.bfloat16)
    grad_gate_w = matmul(normed.T, grad_gate)
    grad_up_w = matmul(normed.T, grad_up)
    grad_normed = matmul(grad_gate, gate_w.T) + matmul(grad_up, up_w.T)
    grad_in, grad_gain = norm_backward(stream, inv_rms, norm_gain, grad_normed)
    return (grad_stream + grad_in, (grad_gain, grad_gate_w, grad_up_w, grad_down))

def group_pass(params, inputs):
    rec_norm_gain, lru_in_weight, gelu_in_weight, conv_weight, gate_a_weight, gate_x_weight, decay_param, lru_out_weight, rec_mlp_gain, rec_mlp_gate, rec_mlp_up, rec_mlp_down, att_norm_gain, query_weight, key_weight, value_weight, att_out_weight, att_mlp_gain, att_mlp_gate, att_mlp_up, att_mlp_down = params
    block_rows, seq_row, cot_rows = inputs
    group_len = seq_row.shape[0]
    lru_width = lru_in_weight.shape[1]
    tap_count = conv_weight.shape[0]
    blocks = gate_a_weight.shape[0]
    block_width = gate_a_weight.shape[1]
    head_size = key_weight.shape[1]
    head_count = query_weight.shape[1] // head_size
    pos_row = positions(seq_row)
    is_start = (pos_row == 0)[:, None]
    stream_zero = block_rows.astype(jnp.float32)
    normed_one, inv_one = norm_forward(stream_zero, rec_norm_gain)
    lru_input = matmul(normed_one, lru_in_weight).astype(jnp.bfloat16)
    conv_taps = conv_weight.astype(jnp.float32).reshape(tap_count, lru_width)
    padded = jnp.concatenate([jnp.zeros((tap_count - 1, lru_width), jnp.bfloat16), lru_input], axis=0)
    conv_sum = jnp.zeros((group_len, lru_width), jnp.float32)
    for tap_index in range(tap_count):
        lagged = padded[tap_count - 1 - tap_index:tap_count - 1 - tap_index + group_len].astype(jnp.float32)
        conv_sum = conv_sum + jnp.where((pos_row >= tap_index)[:, None], conv_taps[tap_index] * lagged, 0.0)
    gate_input = conv_sum.astype(jnp.bfloat16)
    gate_float = gate_input.astype(jnp.float32)
    gate_blocks = gate_float.reshape(group_len, blocks, block_width)
    gate_a_float = gate_a_weight.astype(jnp.float32)
    gate_x_float = gate_x_weight.astype(jnp.float32)
    recall_gate = jax.nn.sigmoid(jnp.einsum('tkc,kcd->tkd', gate_blocks, gate_a_float).reshape(group_len, lru_width))
    input_gate = jax.nn.sigmoid(jnp.einsum('tkc,kcd->tkd', gate_blocks, gate_x_float).reshape(group_len, lru_width))
    decay_float = decay_param.astype(jnp.float32).reshape(lru_width)
    decay_rate = jax.nn.softplus(decay_float)
    decays = jnp.where(is_start, 0.0, jnp.exp(-8.0 * recall_gate * decay_rate))
    input_scale = jnp.sqrt(1.0 - decays * decays)
    driven = input_gate * gate_float * input_scale
    decay_cum, lru_state = linear_scan(decays, driven)
    gelu_pre = matmul(normed_one, gelu_in_weight)
    gelu_out = gelu_fn(gelu_pre)
    mixed = (lru_state * gelu_out).astype(jnp.bfloat16)
    stream_one = stream_zero + matmul(mixed, lru_out_weight)
    stream_two, saved_two = mlp_forward(stream_one, rec_mlp_gain, rec_mlp_gate, rec_mlp_up, rec_mlp_down)
    normed_three, inv_three = norm_forward(stream_two, att_norm_gain)
    cosine, sine_part = rope_tables(pos_row, head_size)
    query_rot = (rotate(matmul(normed_three, query_weight).reshape(group_len, head_count, head_size), cosine, sine_part) * 0.0625).astype(jnp.bfloat16)
    key_rot = rotate(matmul(normed_three, key_weight)[:, None, :], cosine, sine_part)[:, 0, :].astype(jnp.bfloat16)
    value_rows = matmul(normed_three, value_weight).astype(jnp.bfloat16)
    token_index = jnp.arange(group_len, dtype=jnp.int32)
    allowed = (seq_row[:, None] == seq_row[None, :]) & (token_index[None, :] <= token_index[:, None])
    query_float = query_rot.astype(jnp.float32)
    key_float = key_rot.astype(jnp.float32)
    value_float = value_rows.astype(jnp.float32)
    scores = jnp.einsum('thd,kd->htk', query_float, key_float)
    scores = jnp.where(allowed[None], scores, -1e+30)
    log_total = jnp.log(lax.optimization_barrier(jnp.sum(jnp.exp(scores), axis=-1)))
    attn_prob = jnp.exp(scores - log_total[..., None])
    prob_low = attn_prob.astype(jnp.bfloat16)
    att_heads = jnp.einsum('htk,kd->thd', prob_low.astype(jnp.float32), value_float).astype(jnp.bfloat16)
    att_flat = att_heads.reshape(group_len, head_count * head_size)
    stream_three = stream_two + matmul(att_flat, att_out_weight)
    stream_four, saved_four = mlp_forward(stream_three, att_mlp_gain, att_mlp_gate, att_mlp_up, att_mlp_down)
    block_out = stream_four.astype(jnp.bfloat16)
    grad_three, grads_mlp_two = mlp_backward(cot_rows, stream_three, saved_four, att_mlp_gain, att_mlp_gate, att_mlp_up, att_mlp_down)
    grad_three_low = grad_three.astype(jnp.bfloat16)
    grad_att_out = matmul(att_flat.T, grad_three_low)
    grad_heads = matmul(grad_three_low, att_out_weight.T).astype(jnp.bfloat16).reshape(group_len, head_count, head_size)
    grad_heads_float = grad_heads.astype(jnp.float32)
    row_dot = lax.optimization_barrier(jnp.sum(grad_heads_float * att_heads.astype(jnp.float32), axis=-1))
    grad_prob = jnp.einsum('thd,kd->htk', grad_heads_float, value_float)
    grad_scores = (attn_prob * (grad_prob - row_dot.T[:, :, None])).astype(jnp.bfloat16)
    grad_scores_float = grad_scores.astype(jnp.float32)
    grad_values = jnp.einsum('htk,thd->kd', prob_low.astype(jnp.float32), grad_heads_float)
    grad_query = jnp.einsum('htk,kd->thd', grad_scores_float, key_float)
    grad_keys = jnp.einsum('htk,thd->kd', grad_scores_float, query_float)
    grad_query_low = (rotate(grad_query, cosine, -sine_part) * 0.0625).astype(jnp.bfloat16).reshape(group_len, head_count * head_size)
    grad_key_low = rotate(grad_keys[:, None, :], cosine, -sine_part)[:, 0, :].astype(jnp.bfloat16)
    grad_value_low = grad_values.astype(jnp.bfloat16)
    grad_query_w = matmul(normed_three.T, grad_query_low)
    grad_key_w = matmul(normed_three.T, grad_key_low)
    grad_value_w = matmul(normed_three.T, grad_value_low)
    grad_normed_three = matmul(grad_query_low, query_weight.T) + matmul(grad_key_low, key_weight.T) + matmul(grad_value_low, value_weight.T)
    grad_in_three, grad_gain_three = norm_backward(stream_two, inv_three, att_norm_gain, grad_normed_three)
    grad_two = grad_three + grad_in_three
    grad_one, grads_mlp_one = mlp_backward(grad_two, stream_one, saved_two, rec_mlp_gain, rec_mlp_gate, rec_mlp_up, rec_mlp_down)
    grad_one_low = grad_one.astype(jnp.bfloat16)
    grad_out_w = matmul(mixed.T, grad_one_low)
    grad_mixed = matmul(grad_one_low, lru_out_weight.T)
    grad_lru = grad_mixed * gelu_out
    grad_gelu_low = (grad_mixed * lru_state * gelu_slope(gelu_pre)).astype(jnp.bfloat16)
    grad_gelu_w = matmul(normed_one.T, grad_gelu_low)
    next_decay = jnp.concatenate([decays[1:], jnp.ones((1, lru_width), jnp.float32)], axis=0)
    back_cum, back_local = linear_scan(next_decay[::-1], grad_lru[::-1])
    state_grad = back_local[::-1]
    state_before = jnp.concatenate([jnp.zeros((1, lru_width), jnp.float32), lru_state[:-1]], axis=0)
    grad_scale = state_grad * input_gate * gate_float
    grad_decays = jnp.where(is_start, 0.0, state_grad * state_before - grad_scale * decays / input_scale)
    grad_log = grad_decays * decays
    grad_decay = lax.optimization_barrier(jnp.sum(grad_log * -8.0 * recall_gate, axis=0)) * jax.nn.sigmoid(decay_float)
    grad_recall = grad_log * -8.0 * decay_rate
    grad_input_gate = state_grad * gate_float * input_scale
    grad_a_pre = (grad_recall * recall_gate * (1.0 - recall_gate)).astype(jnp.bfloat16).reshape(group_len, blocks, block_width)
    grad_x_pre = (grad_input_gate * input_gate * (1.0 - input_gate)).astype(jnp.bfloat16).reshape(group_len, blocks, block_width)
    grad_a_float = grad_a_pre.astype(jnp.float32)
    grad_x_float = grad_x_pre.astype(jnp.float32)
    grad_gate_a = jnp.einsum('tkc,tkd->kcd', gate_blocks, grad_a_float)
    grad_gate_x = jnp.einsum('tkc,tkd->kcd', gate_blocks, grad_x_float)
    conv_grad = state_grad * input_gate * input_scale + jnp.einsum('tkd,kcd->tkc', grad_a_float, gate_a_float).reshape(group_len, lru_width) + jnp.einsum('tkd,kcd->tkc', grad_x_float, gate_x_float).reshape(group_len, lru_width)
    padded_grad = jnp.concatenate([conv_grad, jnp.zeros((tap_count - 1, lru_width), jnp.float32)], axis=0)
    padded_pos = jnp.concatenate([pos_row.astype(jnp.int32), jnp.full((tap_count - 1,), -1, jnp.int32)])
    grad_input = jnp.zeros((group_len, lru_width), jnp.float32)
    tap_grads = []
    for tap_index in range(tap_count):
        lagged = padded[tap_count - 1 - tap_index:tap_count - 1 - tap_index + group_len].astype(jnp.float32)
        tap_grads.append(lax.optimization_barrier(jnp.sum(jnp.where((pos_row >= tap_index)[:, None], conv_grad * lagged, 0.0), axis=0)))
        ahead = padded_grad[tap_index:tap_index + group_len]
        grad_input = grad_input + jnp.where((padded_pos[tap_index:tap_index + group_len] >= tap_index)[:, None], conv_taps[tap_index] * ahead, 0.0)
    grad_conv = jnp.stack(tap_grads).reshape(tap_count, blocks, block_width)
    grad_input_low = grad_input.astype(jnp.bfloat16)
    grad_in_w = matmul(normed_one.T, grad_input_low)
    grad_normed_one = matmul(grad_input_low, lru_in_weight.T) + matmul(grad_gelu_low, gelu_in_weight.T)
    grad_in_zero, grad_gain_one = norm_backward(stream_zero, inv_one, rec_norm_gain, grad_normed_one)
    grad_zero = grad_one + grad_in_zero
    grads = (grad_gain_one, grad_in_w, grad_gelu_w, grad_conv, grad_gate_a, grad_gate_x, grad_decay.reshape(blocks, block_width), grad_out_w, grads_mlp_one[0], grads_mlp_one[1], grads_mlp_one[2], grads_mlp_one[3], grad_gain_three, grad_query_w, grad_key_w, grad_value_w, grad_att_out, grads_mlp_two[0], grads_mlp_two[1], grads_mlp_two[2], grads_mlp_two[3])
    return (block_out, grad_zero, grads)

def reference(block_input, seq_ids, out_cotangent, rec_norm_gain, lru_in_weight, gelu_in_weight, conv_weight, gate_a_weight, gate_x_weight, decay_param, lru_out_weight, rec_mlp_gain, rec_mlp_gate, rec_mlp_up, rec_mlp_down, att_norm_gain, query_weight, key_weight, value_weight, att_out_weight, att_mlp_gain, att_mlp_gate, att_mlp_up, att_mlp_down):
    params = (rec_norm_gain, lru_in_weight, gelu_in_weight, conv_weight, gate_a_weight, gate_x_weight, decay_param, lru_out_weight, rec_mlp_gain, rec_mlp_gate, rec_mlp_up, rec_mlp_down, att_norm_gain, query_weight, key_weight, value_weight, att_out_weight, att_mlp_gain, att_mlp_gate, att_mlp_up, att_mlp_down)
    block_groups = block_input.reshape(N_DP, S, D)
    cot_groups = out_cotangent.reshape(N_DP, S, D)
    zero_grads = tuple((jnp.zeros(param_arr.shape, jnp.float32) for param_arr in params))

    def step_fn(totals, inputs):
        out_rows, grad_rows, grads = group_pass(params, inputs)
        return (tuple((total_arr + grad_arr for total_arr, grad_arr in zip(totals, grads))), (out_rows, grad_rows))
    totals, stacked = lax.scan(step_fn, zero_grads, (block_groups, seq_ids, cot_groups))
    return (stacked[0].reshape(TOKENS, D), stacked[1].reshape(TOKENS, D), totals[0], totals[1], totals[2], totals[3], totals[4], totals[5], totals[6], totals[7], totals[8], totals[9], totals[10], totals[11], totals[12], totals[13], totals[14], totals[15], totals[16], totals[17], totals[18], totals[19], totals[20])
```

```python
import jax
import jax.numpy as jnp
from jax import lax
from jax.experimental import pallas as pl
from jax.experimental.pallas import tpu as pltpu
from jax.sharding import PartitionSpec as P

norm_epsilon = 1e-06
bf16 = jnp.bfloat16
f32 = jnp.float32


def swap(x, bit):
    peers = lax.axis_size("dp")
    return lax.ppermute(x, "dp", [(i, i ^ bit) for i in range(peers)])


def shift(x, by):
    peers = lax.axis_size("seq")
    pairs = [(i, i + by) for i in range(peers) if 0 <= i + by < peers]
    return lax.ppermute(x, "seq", pairs)


def partner(x):
    peers = lax.axis_size("tensor")
    return lax.ppermute(x, "tensor", [(i, peers - 1 - i) for i in range(peers)])


def both_cores(x):
    low = x.astype(bf16)
    return low.astype(f32) + partner(low).astype(f32)


def bit_orders():
    bits = []
    while (1 << len(bits)) < lax.axis_size("dp"):
        bits.append(1 << len(bits))
    return bits, bits[1:] + bits[:1]


def rows_of(x, r, tokens):
    return x[r * tokens : (r + 1) * tokens]


def scatter_sum(blocks, product, order):
    tokens = blocks[0].shape[0]
    held = {r: [] for r in range(len(blocks))}
    left = list(range(len(blocks)))
    for bit in order:
        away = [r for r in left if r & bit]
        left = [r for r in left if not r & bit]
        part = product(jnp.concatenate([blocks[r] for r in away]))
        for k in range(len(held[away[0]])):
            part = part + jnp.concatenate([held[r][k] for r in away]).astype(f32)
        got = swap(part.astype(bf16), bit)
        for i, r in enumerate(away):
            held[r ^ bit].append(rows_of(got, i, tokens))
    total = product(blocks[0])
    for piece in held[0]:
        total = total + piece.astype(f32)
    return total


def spread(block, order):
    blocks = {0: block}
    for bit in order:
        blocks.update({r ^ bit: swap(b, bit) for r, b in list(blocks.items())})
    return jnp.concatenate([blocks[r] for r in range(len(blocks))])


def owner_sum(rows):
    total = rows[0:1]
    for r in range(1, rows.shape[0]):
        total = total + swap(rows[r : r + 1], r)
    return total


def spread_row(row):
    return jnp.concatenate([row] + [swap(row, r) for r in range(1, lax.axis_size("dp"))])


def to_slices(rows):
    peers = lax.axis_size("dp")
    place = lax.axis_index("dp")
    width = rows.shape[1] // peers
    out = []
    for r in range(peers):
        piece = lax.dynamic_slice_in_dim(rows, (place ^ r) * width, width, axis=1)
        out.append(swap(piece, r) if r else piece)
    return jnp.concatenate(out)


def to_rows(slices):
    peers = lax.axis_size("dp")
    place = lax.axis_index("dp")
    tokens = slices.shape[0] // peers
    width = slices.shape[1]
    out = jnp.zeros((tokens, width * peers), slices.dtype)
    for r in range(peers):
        piece = rows_of(slices, r, tokens)
        piece = swap(piece, r) if r else piece
        out = lax.dynamic_update_slice_in_dim(out, piece, (place ^ r) * width, axis=1)
    return out


def seq_sum(part):
    peers = lax.axis_size("seq")
    low = part.astype(bf16)
    if peers != 4:
        return lax.psum(low, "seq").astype(f32)
    place = lax.axis_index("seq")
    inner = (place == 1) | (place == 2)
    got = lax.ppermute(low, "seq", [(0, 1), (3, 2)])
    half = (low.astype(f32) + got.astype(f32)).astype(bf16)
    got = lax.ppermute(half, "seq", [(1, 2), (2, 1)])
    total = (half.astype(f32) + got.astype(f32)).astype(bf16)
    got = lax.ppermute(total, "seq", [(1, 0), (2, 3)])
    return jnp.where(inner, total, got).astype(f32)


def matmul(left, right):
    return jnp.dot(left, right, preferred_element_type=f32)


def matmul_t(left, right):
    return lax.dot_general(left, right, (((1,), (1,)), ((), ())), preferred_element_type=f32)


def t_matmul(left, right):
    return lax.dot_general(left, right, (((0,), (0,)), ((), ())), preferred_element_type=f32)


def gelu_fn(values):
    return jax.nn.gelu(values, approximate=True)


def gelu_slope(values):
    return jax.vjp(gelu_fn, values)[1](jnp.ones_like(values))[0]


def cuts(width):
    tiles = width // 128
    if tiles < 2 or width % 128:
        half = (width + 1) // 2
    else:
        half = (tiles + 1) // 2 * 128
    return ((0, half), (half, width))


def positions(seq_row):
    token_index = jnp.arange(seq_row.shape[0], dtype=jnp.int32)
    earlier = jnp.concatenate([seq_row[:1] - 1, seq_row[:-1]])
    seg_first = jnp.where(seq_row != earlier, token_index, jnp.zeros_like(token_index))
    return token_index - lax.cummax(seg_first, axis=0)


def rope_tables(pos_row, head_size):
    half_size = head_size // 2
    freqs = jnp.exp(
        -jnp.log(10000.0) * (2.0 * jnp.arange(half_size).astype(f32) / head_size)
    )
    angles = pos_row.astype(f32)[:, None] * freqs[None, :]
    return (jnp.cos(angles), jnp.sin(angles))


def rotate(vectors, cosine, sine_part):
    half_size = vectors.shape[-1] // 2
    first_half = vectors[..., :half_size]
    second_half = vectors[..., half_size:]
    cos_b = cosine[:, None, :]
    sin_b = sine_part[:, None, :]
    return jnp.concatenate(
        [first_half * cos_b - second_half * sin_b, second_half * cos_b + first_half * sin_b],
        axis=-1,
    )


def scan_body(decay_ref, value_ref, state_ref, cum_ref, *, reverse):
    length, width = decay_ref.shape
    tiles = length // 8
    row = lax.broadcasted_iota(jnp.int32, (8, width), 0)

    def one(step, carry):
        cum, state = carry
        tile = tiles - 1 - step if reverse else step
        at = pl.ds(pl.multiple_of(tile * 8, 8), 8)
        decay = decay_ref[at, :]
        value = value_ref[at, :]
        for lag in (1, 2, 4):
            if reverse:
                known = row < 8 - lag
                turn = 8 - lag
            else:
                known = row >= lag
                turn = lag
            before_decay = jnp.where(known, pltpu.roll(decay, turn, 0), 1.0)
            before_value = jnp.where(known, pltpu.roll(value, turn, 0), 0.0)
            value = value + decay * before_value
            decay = decay * before_decay
        value = value + decay * state
        decay = decay * cum
        state_ref[at, :] = value
        cum_ref[at, :] = decay
        last = slice(0, 1) if reverse else slice(7, 8)
        return (decay[last], value[last])

    lax.fori_loop(
        0, tiles, one, (jnp.ones((1, width), f32), jnp.zeros((1, width), f32)), unroll=2
    )


def linear_scan(decays, values, reverse):
    def body(decay_ref, value_ref, state_ref, cum_ref):
        scan_body(decay_ref, value_ref, state_ref, cum_ref, reverse=reverse)

    shape = jax.ShapeDtypeStruct(decays.shape, f32)
    state, cum = pl.pallas_call(
        body,
        out_shape=(shape, shape),
        in_specs=[pl.BlockSpec(memory_space=pltpu.VMEM)] * 2,
        out_specs=[pl.BlockSpec(memory_space=pltpu.VMEM)] * 2,
        cost_estimate=pl.CostEstimate(
            flops=20 * decays.size, bytes_accessed=16 * decays.size, transcendentals=0
        ),
        name="scan_back" if reverse else "scan_ahead",
    )(decays, values)
    return cum, state


def carried_in(cum_edge, state_edge, toward):
    pair = jnp.stack([cum_edge, state_edge])
    pieces = [shift(pair, toward * k) for k in range(1, lax.axis_size("seq"))]
    state = jnp.zeros_like(state_edge)
    for piece in reversed(pieces):
        state = piece[1] + piece[0] * state
    return state


def norm_start(stream, gain, tokens):
    scaled = (stream * gain.astype(f32)).astype(bf16)
    squares = jnp.sum(stream * stream, axis=1).reshape(-1, tokens)
    return scaled, owner_sum(squares)


def inverse_rms(squares, width):
    return lax.rsqrt(squares[0] / width + norm_epsilon)[:, None]


def split_rows(x, tokens):
    return [rows_of(x, r, tokens) for r in range(x.shape[0] // tokens)]


def join_weights(gate_w, up_w):
    return [
        jnp.concatenate([gate_w[:, a:b], up_w[:, a:b]], axis=1) for a, b in cuts(gate_w.shape[1])
    ]


def mlp_forward(stream, gain, joined, down_w, tokens, width):
    orders = bit_orders()
    scaled, squares = norm_start(stream, gain, tokens)
    blocks = split_rows(scaled, tokens)
    pres = [
        scatter_sum(blocks, lambda x, w=w: matmul(x, w), order)
        for w, order in zip(joined, orders)
    ]
    inv = inverse_rms(squares, width)
    hidden, total = [], 0.0
    acts = []
    for pre, (a, b), order in zip(pres, cuts(down_w.shape[0]), orders[::-1]):
        pre = pre * inv
        gate, up = pre[:, : b - a], pre[:, b - a :]
        acts.append((gate, up))
        every = spread((gelu_fn(gate) * up).astype(bf16), order)
        hidden.append(every)
        total = total + matmul(every, down_w[a:b])
    return stream + both_cores(total), (scaled, inv, acts, hidden)


def norm_finish(grad_stream, stream, gain, grad_scaled, pull):
    weighted = grad_scaled * gain.astype(f32)
    grad_gain = jnp.sum(grad_scaled * stream, axis=0)
    change = weighted - stream * pull.reshape(-1)[:, None]
    return grad_stream + both_cores(change), grad_gain


def mlp_backward(grad_stream, stream, saved, gain, joined, down_w, tokens, width):
    orders = bit_orders()
    scaled, inv, acts, hidden = saved
    low = grad_stream.astype(bf16)
    blocks = split_rows(low, tokens)
    sides = cuts(down_w.shape[0])
    grad_hidden = [
        scatter_sum(blocks, lambda x, w=down_w[a:b]: matmul_t(x, w), order)
        for (a, b), order in zip(sides, orders)
    ]
    grad_down = [t_matmul(every, low) for every in hidden]
    grad_joined, grad_scaled, pull = [], 0.0, 0.0
    for gh, (gate, up), w, order in zip(grad_hidden, acts, joined, orders[::-1]):
        gh = gh * inv
        back = jnp.concatenate(
            [(gh * up * gelu_slope(gate)).astype(bf16), (gh * gelu_fn(gate)).astype(bf16)], axis=1
        )
        half = gate.shape[1]
        pull = pull + jnp.sum(
            back[:, :half].astype(f32) * gate + back[:, half:].astype(f32) * up, axis=1
        )
        every = spread(back, order)
        grad_joined.append(t_matmul(scaled, every))
        grad_scaled = grad_scaled + matmul_t(every, w)
    pull = spread_row((pull * inv[:, 0] / width)[None])
    grad_in, grad_gain = norm_finish(grad_stream, stream, gain, grad_scaled, pull)
    return grad_in, grad_gain, grad_joined, grad_down


def finish_mlp(grad_joined, grad_down):
    sums = [seq_sum(g) for g in grad_joined]
    gate = jnp.concatenate([g[:, : g.shape[1] // 2] for g in sums], axis=1)
    up = jnp.concatenate([g[:, g.shape[1] // 2 :] for g in sums], axis=1)
    return gate, up, jnp.concatenate([seq_sum(g) for g in grad_down], axis=0)


def local(
    block_input,
    seq_ids,
    out_cotangent,
    rec_norm_gain,
    lru_in_weight,
    gelu_in_weight,
    conv_weight,
    gate_a_weight,
    gate_x_weight,
    decay_param,
    lru_out_weight,
    rec_mlp_gain,
    rec_mlp_gate,
    rec_mlp_up,
    rec_mlp_down,
    att_norm_gain,
    query_weight,
    key_weight,
    value_weight,
    att_out_weight,
    att_mlp_gain,
    att_mlp_gate,
    att_mlp_up,
    att_mlp_down,
):
    tokens, width = block_input.shape
    pieces = lax.axis_size("seq")
    piece_at = lax.axis_index("seq")
    first_core = lax.axis_index("tensor") == 0
    orders = bit_orders()
    group_row = seq_ids[0]
    span_start = piece_at * tokens
    group_pos = positions(group_row)
    local_pos = lax.dynamic_slice_in_dim(group_pos, span_start, tokens)
    local_ids = lax.dynamic_slice_in_dim(group_row, span_start, tokens)
    is_start = (local_pos == 0)[:, None]

    blocks_here, _, block_width = gate_a_weight.shape
    tap_count = conv_weight.shape[0]
    gates_full = lax.all_gather(
        jnp.concatenate([gate_a_weight, gate_x_weight]), "dp", axis=1, tiled=True
    )
    gate_a_full, gate_x_full = gates_full[:blocks_here], gates_full[blocks_here:]
    channel_full = lax.all_gather(
        jnp.concatenate([conv_weight, decay_param[None]]), "dp", axis=2, tiled=True
    )
    conv_full, decay_full = channel_full[:tap_count], channel_full[tap_count]
    lru_width = lru_in_weight.shape[1]

    joined_one = join_weights(rec_mlp_gate, rec_mlp_up)
    joined_two = join_weights(att_mlp_gate, att_mlp_up)

    own_rows = block_input.astype(f32)
    inv_one = lax.rsqrt(jnp.mean(own_rows * own_rows, axis=-1, keepdims=True) + norm_epsilon)
    stream_zero = to_slices(block_input).astype(f32)
    scaled_one = (stream_zero * rec_norm_gain.astype(f32)).astype(bf16)
    blocks_one = split_rows(scaled_one, tokens)
    lru_cuts = cuts(lru_width)

    def in_branch(weight):
        return inv_one * jnp.concatenate(
            [
                scatter_sum(blocks_one, lambda x, w=weight[:, a:b]: matmul(x, w), order)
                for (a, b), order in zip(lru_cuts, orders)
            ],
            axis=1,
        )

    lru_pre = in_branch(lru_in_weight)
    gelu_pre = in_branch(gelu_in_weight)
    lru_input = lru_pre.astype(bf16)
    conv_taps = conv_full.astype(f32).reshape(tap_count, lru_width)
    rim_rows = shift(lru_input[tokens - (tap_count - 1) :], 1)
    padded = jnp.concatenate([rim_rows, lru_input], axis=0)
    conv_sum = jnp.zeros((tokens, lru_width), f32)
    for tap in range(tap_count):
        lagged = padded[tap_count - 1 - tap : tap_count - 1 - tap + tokens].astype(f32)
        conv_sum = conv_sum + jnp.where(
            (local_pos >= tap)[:, None], conv_taps[tap] * lagged, 0.0
        )
    gate_input = conv_sum.astype(bf16)
    gate_float = gate_input.astype(f32)

    def by_block(x, weight, product):
        return jnp.concatenate(
            [
                product(x[:, k * block_width : (k + 1) * block_width], weight[k])
                for k in range(blocks_here)
            ],
            axis=1,
        )

    recall_gate = jax.nn.sigmoid(by_block(gate_input, gate_a_full, matmul))
    input_gate = jax.nn.sigmoid(by_block(gate_input, gate_x_full, matmul))
    decay_float = decay_full.astype(f32).reshape(lru_width)
    decay_rate = jax.nn.softplus(decay_float)
    decays = jnp.where(is_start, 0.0, jnp.exp(-8.0 * recall_gate * decay_rate))
    input_scale = jnp.sqrt(1.0 - decays * decays)
    driven = input_gate * gate_float * input_scale
    decay_cum, state_local = linear_scan(decays, driven, False)
    carry_state = carried_in(decay_cum[-1], state_local[-1], 1)
    lru_state = state_local + decay_cum * carry_state[None, :]
    gelu_out = gelu_fn(gelu_pre)
    mixed_own = (lru_state * gelu_out).astype(bf16)
    mixed = [spread(mixed_own[:, a:b], order) for (a, b), order in zip(lru_cuts, orders)]
    branch = sum(matmul(every, lru_out_weight[a:b]) for every, (a, b) in zip(mixed, lru_cuts))
    stream_one = stream_zero + both_cores(branch)

    stream_two, saved_two = mlp_forward(
        stream_one, rec_mlp_gain, joined_one, rec_mlp_down, tokens, width
    )

    head_size = key_weight.shape[1]
    heads_here = query_weight.shape[1] // head_size
    early_heads = max(heads_here - 1, 0) // 2
    edge = early_heads * head_size
    pair_weight = jnp.where(first_core, key_weight, value_weight)
    qkv_weights = [
        jnp.concatenate([pair_weight, query_weight[:, :edge]], axis=1),
        query_weight[:, edge:],
    ]
    scaled_three, squares_three = norm_start(stream_two, att_norm_gain, tokens)
    blocks_three = split_rows(scaled_three, tokens)
    qkv_pre = [
        scatter_sum(blocks_three, lambda x, w=w: matmul(x, w), order)
        for w, order in zip(qkv_weights, orders)
    ]
    inv_three = inverse_rms(squares_three, width)
    qkv_pre = [inv_three * pre for pre in qkv_pre]
    cosine, sine_part = rope_tables(local_pos, head_size)
    pair_pre = qkv_pre[0][:, :head_size]
    query_pre = jnp.concatenate([qkv_pre[0][:, head_size:], qkv_pre[1]], axis=1)
    query_rot = (
        rotate(query_pre.reshape(tokens, heads_here, head_size), cosine, sine_part) * 0.0625
    ).astype(bf16)
    pair_own = jnp.where(
        first_core, rotate(pair_pre[:, None, :], cosine, sine_part)[:, 0, :], pair_pre
    ).astype(bf16)
    pair_all = jnp.concatenate([pair_own] + [shift(pair_own, k) for k in range(1, pieces)])
    pair_other = partner(pair_all)
    keys_all = jnp.where(first_core, pair_all, pair_other)
    values_all = jnp.where(first_core, pair_other, pair_all)
    token_at = jnp.arange(tokens, dtype=jnp.int32)
    query_index = span_start + token_at
    key_index = jnp.concatenate([(piece_at - k) * tokens + token_at for k in range(pieces)])
    key_ids = jnp.concatenate(
        [
            lax.dynamic_slice_in_dim(group_row, jnp.maximum(piece_at - k, 0) * tokens, tokens)
            for k in range(pieces)
        ]
    )
    allowed = (
        (local_ids[:, None] == key_ids[None, :])
        & (key_index[None, :] <= query_index[:, None])
        & (key_index >= 0)[None, :]
    )
    scores = jnp.einsum("thd,kd->htk", query_rot, keys_all, preferred_element_type=f32)
    scores = jnp.where(allowed[None], scores, -1e30)
    log_total = jnp.log(jnp.sum(jnp.exp(scores), axis=-1))
    attn_prob = jnp.exp(scores - log_total[..., None])
    prob_low = attn_prob.astype(bf16)
    att_heads = jnp.einsum("htk,kd->thd", prob_low, values_all, preferred_element_type=f32).astype(
        bf16
    )
    att_own = att_heads.reshape(tokens, heads_here * head_size)
    att_cuts = cuts(heads_here * head_size)
    att_flat = [spread(att_own[:, a:b], order) for (a, b), order in zip(att_cuts, orders)]
    branch = sum(matmul(every, att_out_weight[a:b]) for every, (a, b) in zip(att_flat, att_cuts))
    stream_three = stream_two + both_cores(branch)

    stream_four, saved_four = mlp_forward(
        stream_three, att_mlp_gain, joined_two, att_mlp_down, tokens, width
    )
    block_output = to_rows(stream_four.astype(bf16))

    grad_four = to_slices(out_cotangent.astype(bf16)).astype(f32)
    grad_three, grad_gain_four, grad_joined_two, grad_down_two = mlp_backward(
        grad_four, stream_three, saved_four, att_mlp_gain, joined_two, att_mlp_down, tokens, width
    )
    out_mlp_two = finish_mlp(grad_joined_two, grad_down_two)

    low_three = grad_three.astype(bf16)
    blocks_low = split_rows(low_three, tokens)
    grad_heads = jnp.concatenate(
        [
            scatter_sum(blocks_low, lambda x, w=att_out_weight[a:b]: matmul_t(x, w), order)
            for (a, b), order in zip(att_cuts, orders)
        ],
        axis=1,
    )
    out_att_out = jnp.concatenate([seq_sum(t_matmul(every, low_three)) for every in att_flat])
    grad_heads = grad_heads.astype(bf16).reshape(tokens, heads_here, head_size)
    row_dot = jnp.sum(grad_heads.astype(f32) * att_heads.astype(f32), axis=-1)
    grad_prob = jnp.einsum("thd,kd->htk", grad_heads, values_all, preferred_element_type=f32)
    grad_scores = (attn_prob * (grad_prob - row_dot.T[:, :, None])).astype(bf16)
    grad_values_all = jnp.einsum("htk,thd->kd", prob_low, grad_heads, preferred_element_type=f32)
    grad_query = jnp.einsum("htk,kd->thd", grad_scores, keys_all, preferred_element_type=f32)
    grad_keys_all = jnp.einsum("htk,thd->kd", grad_scores, query_rot, preferred_element_type=f32)
    grad_pair = jnp.where(first_core, grad_keys_all, grad_values_all)
    grad_send = jnp.where(first_core, grad_values_all, grad_keys_all)
    grad_pair = (grad_pair + partner(grad_send.astype(bf16)).astype(f32)).astype(bf16)
    grad_pair_own = rows_of(grad_pair, 0, tokens).astype(f32)
    for k in range(1, pieces):
        grad_pair_own = grad_pair_own + shift(rows_of(grad_pair, k, tokens), -k).astype(f32)
    grad_pair_pre = jnp.where(
        first_core,
        rotate(grad_pair_own[:, None, :], cosine, -sine_part)[:, 0, :],
        grad_pair_own,
    )
    grad_query_pre = (rotate(grad_query, cosine, -sine_part) * 0.0625).reshape(
        tokens, heads_here * head_size
    )
    qkv_back = [
        (inv_three * jnp.concatenate([grad_pair_pre, grad_query_pre[:, :edge]], axis=1)).astype(
            bf16
        ),
        (inv_three * grad_query_pre[:, edge:]).astype(bf16),
    ]
    pull = sum(jnp.sum(b.astype(f32) * p, axis=1) for b, p in zip(qkv_back, qkv_pre))
    qkv_every = [None, None]
    for at in (1, 0):
        qkv_every[at] = spread(qkv_back[at], orders[at])
    pull = spread_row((pull * inv_three[:, 0] / width)[None])
    grad_scaled = sum(matmul_t(every, w) for every, w in zip(qkv_every, qkv_weights))
    grad_two, grad_gain_three = norm_finish(
        grad_three, stream_two, att_norm_gain, grad_scaled, pull
    )
    grad_qkv = [seq_sum(t_matmul(scaled_three, every)) for every in qkv_every]
    grad_pair_w = grad_qkv[0][:, :head_size]
    grad_pair_other = partner(grad_pair_w.astype(bf16)).astype(f32)
    out_key = jnp.where(first_core, grad_pair_w, grad_pair_other)
    out_value = jnp.where(first_core, grad_pair_other, grad_pair_w)
    out_query = jnp.concatenate([grad_qkv[0][:, head_size:], grad_qkv[1]], axis=1)

    grad_one, grad_gain_two, grad_joined_one, grad_down_one = mlp_backward(
        grad_two, stream_one, saved_two, rec_mlp_gain, joined_one, rec_mlp_down, tokens, width
    )
    out_mlp_one = finish_mlp(grad_joined_one, grad_down_one)

    low_one = grad_one.astype(bf16)
    blocks_low = split_rows(low_one, tokens)
    grad_mixed = jnp.concatenate(
        [
            scatter_sum(blocks_low, lambda x, w=lru_out_weight[a:b]: matmul_t(x, w), order)
            for (a, b), order in zip(lru_cuts, orders)
        ],
        axis=1,
    )
    out_lru_out = jnp.concatenate([seq_sum(t_matmul(every, low_one)) for every in mixed])
    grad_lru = grad_mixed * gelu_out
    gelu_back = (inv_one * (grad_mixed * lru_state * gelu_slope(gelu_pre))).astype(bf16)
    gelu_every = [spread(gelu_back[:, a:b], order) for (a, b), order in zip(lru_cuts, orders)]
    next_decay = jnp.concatenate([decays[1:], jnp.ones((1, lru_width), f32)], axis=0)
    back_cum, back_local = linear_scan(next_decay, grad_lru, True)
    carry_grad = carried_in(back_cum[0] * decays[0], decays[0] * back_local[0], -1)
    state_grad = back_local + back_cum * carry_grad[None, :]
    state_before = jnp.concatenate([carry_state[None, :], lru_state[:-1]], axis=0)
    grad_scale = state_grad * input_gate * gate_float
    grad_decays = jnp.where(
        is_start, 0.0, state_grad * state_before - grad_scale * decays / input_scale
    )
    grad_log = grad_decays * decays
    grad_decay = jnp.sum(grad_log * -8.0 * recall_gate, axis=0) * jax.nn.sigmoid(decay_float)
    grad_recall = grad_log * -8.0 * decay_rate
    grad_input_gate = state_grad * gate_float * input_scale
    grad_a_pre = (grad_recall * recall_gate * (1.0 - recall_gate)).astype(bf16)
    grad_x_pre = (grad_input_gate * input_gate * (1.0 - input_gate)).astype(bf16)
    conv_grad = (
        state_grad * input_gate * input_scale
        + by_block(grad_a_pre, gate_a_full, matmul_t)
        + by_block(grad_x_pre, gate_x_full, matmul_t)
    )
    next_rows = shift(conv_grad[: tap_count - 1], -1)
    padded_grad = jnp.concatenate([conv_grad, next_rows], axis=0)
    group_pos_pad = jnp.concatenate([group_pos, jnp.full((tap_count - 1,), -1, jnp.int32)])
    padded_pos = lax.dynamic_slice_in_dim(group_pos_pad, span_start, tokens + tap_count - 1)
    grad_input = jnp.zeros((tokens, lru_width), f32)
    tap_grads = []
    for tap in range(tap_count):
        lagged = padded[tap_count - 1 - tap : tap_count - 1 - tap + tokens].astype(f32)
        tap_grads.append(
            jnp.sum(jnp.where((local_pos >= tap)[:, None], conv_grad * lagged, 0.0), axis=0)
        )
        grad_input = grad_input + jnp.where(
            (padded_pos[tap : tap + tokens] >= tap)[:, None],
            conv_taps[tap] * padded_grad[tap : tap + tokens],
            0.0,
        )
    lru_back = (inv_one * grad_input).astype(bf16)
    lru_every = [spread(lru_back[:, a:b], order) for (a, b), order in zip(lru_cuts, orders)]
    pull = jnp.sum(gelu_back.astype(f32) * gelu_pre + lru_back.astype(f32) * lru_pre, axis=1)
    pull = spread_row((pull * inv_one[:, 0] / width)[None])
    grad_scaled = sum(
        matmul_t(every, gelu_in_weight[:, a:b]) for every, (a, b) in zip(gelu_every, lru_cuts)
    ) + sum(matmul_t(every, lru_in_weight[:, a:b]) for every, (a, b) in zip(lru_every, lru_cuts))
    grad_zero, grad_gain_one = norm_finish(
        grad_one, stream_zero, rec_norm_gain, grad_scaled, pull
    )
    input_grad = to_rows(grad_zero.astype(bf16)).astype(f32)
    out_gelu_in = jnp.concatenate(
        [seq_sum(t_matmul(scaled_one, every)) for every in gelu_every], axis=1
    )
    out_lru_in = jnp.concatenate(
        [seq_sum(t_matmul(scaled_one, every)) for every in lru_every], axis=1
    )

    def block_grads(back):
        return jnp.stack(
            [
                t_matmul(
                    gate_input[:, k * block_width : (k + 1) * block_width],
                    back[:, k * block_width : (k + 1) * block_width],
                )
                for k in range(blocks_here)
            ]
        )

    grad_gates = lax.psum_scatter(
        jnp.concatenate([block_grads(grad_a_pre), block_grads(grad_x_pre)]).astype(bf16),
        "dp",
        scatter_dimension=1,
        tiled=True,
    )
    out_gates = seq_sum(grad_gates)
    grad_channels = lax.psum_scatter(
        jnp.concatenate([jnp.stack(tap_grads), grad_decay[None]]).reshape(
            tap_count + 1, blocks_here, block_width
        ),
        "dp",
        scatter_dimension=2,
        tiled=True,
    )
    out_channels = lax.psum(grad_channels, "seq")
    out_gains = lax.psum(
        jnp.stack([grad_gain_one, grad_gain_two, grad_gain_three, grad_gain_four]),
        ("seq", "tensor"),
    )
    return (
        block_output,
        input_grad,
        out_gains[0],
        out_lru_in,
        out_gelu_in,
        out_channels[:tap_count],
        out_gates[:blocks_here],
        out_gates[blocks_here:],
        out_channels[tap_count],
        out_lru_out,
        out_gains[1],
        *out_mlp_one,
        out_gains[2],
        out_query,
        out_key,
        out_value,
        out_att_out,
        out_gains[3],
        *out_mlp_two,
    )


def solution(mesh):
    return jax.shard_map(
        local,
        mesh=mesh,
        in_specs=(
            P(("dp", "seq"), None),
            P("dp", None),
            P(("dp", "seq"), None),
            P("dp"),
            P("dp", "tensor"),
            P("dp", "tensor"),
            P(None, "tensor", "dp"),
            P("tensor", "dp", None),
            P("tensor", "dp", None),
            P("tensor", "dp"),
            P("tensor", "dp"),
            P("dp"),
            P("dp", "tensor"),
            P("dp", "tensor"),
            P("tensor", "dp"),
            P("dp"),
            P("dp", "tensor"),
            P("dp", None),
            P("dp", None),
            P("tensor", "dp"),
            P("dp"),
            P("dp", "tensor"),
            P("dp", "tensor"),
            P("tensor", "dp"),
        ),
        out_specs=(
            P(("dp", "seq"), None),
            P(("dp", "seq"), None),
            P("dp"),
            P("dp", "tensor"),
            P("dp", "tensor"),
            P(None, "tensor", "dp"),
            P("tensor", "dp", None),
            P("tensor", "dp", None),
            P("tensor", "dp"),
            P("tensor", "dp"),
            P("dp"),
            P("dp", "tensor"),
            P("dp", "tensor"),
            P("tensor", "dp"),
            P("dp"),
            P("dp", "tensor"),
            P("dp", None),
            P("dp", None),
            P("tensor", "dp"),
            P("dp"),
            P("dp", "tensor"),
            P("dp", "tensor"),
            P("tensor", "dp"),
        ),
        check_vma=False,
    )
```
